32 devices in a mesh: grp: 2 (over x), ty: 16 (over z, y, core).
Axes of the slice: x: 2, y: 2, z: 4, core: 2. Of those that a mesh axis runs over, the one named last changes fastest.
Arguments:
- tile_object: float32 [4, 2, 4096, 768], P(None, None, ('grp', 'ty')), parts along dimension 2, may hold values from -6 to 6
- probe_wave: float32 [2, 128, 128], replicated, may hold values from -6 to 6
- propagator_phase: float32 [128, 128], replicated, may hold values from -3.140625 to 3.140625
- diffraction: float32 [128, 128, 128], P(('grp', 'ty')), parts along dimension 0, may hold values from 0 to 2
- positions: int32 [128, 2], P(('grp', 'ty')), parts along dimension 0, may hold values from 0 to 640, as said below
- counts: int32 [32], P(('grp', 'ty')), parts along dimension 0, may hold values from 0 to 4, as said below
Outputs:
- object_grad: float32 [4, 2, 4096, 768], P(None, None, ('grp', 'ty')), parts along dimension 2
The draws below stay inside these ranges and needn't reach their ends.
There are 2 independent parts, one for each index of `grp`. The reference program is written for one: setup_inputs(seed, part) draws one part's arguments, and reference() takes and returns one part's arrays. A program takes and returns all parts, laid end to end along the dimension named above; an argument that names none is the same for every part. Nothing has to cross between parts.
Inputs may be any that keep to these rules, and one draw needn't show every extreme that they name: `positions`: column 0 is a row offset under 128, column 1 a column offset of at most 640. For every device d, the counts of devices 0 to d sum to between 2 * (d + 1) and 2 * (d + 2), the upper bound reached at some device; all counts sum to 32.
All inputs are finite; a program needn't handle non-finite values.
Results may differ from the reference program's by a relative error of at most 0.0003.
Values sent between devices are 32-bit elements; how exact they have to be, the bound alone decides.
A program may use at most 64 MiB of HBM per device.

```python
import jax
import jax.numpy as jnp
from jax import lax

PS = 128
NS = 4
TR = 128
OW = 768
BATCH = 2
SLOTS = 4
TILES = 16
SLOTS_ALL = 64
OROWS = 2048


def draw_counts(key, part):
    surplus = jax.random.randint(jax.random.fold_in(key, 11), (TILES,), 0, BATCH + 1)
    marker = jax.random.randint(jax.random.fold_in(key, 12), (), 0, TILES - 2)
    indices = jnp.arange(TILES)
    surplus = jnp.where(indices == marker, BATCH, surplus)
    cleared = (indices == marker - 1) | (indices == marker + 1) | (indices == TILES - 1)
    surplus = jnp.where(cleared, 0, surplus)
    before = jnp.concatenate([jnp.zeros((1,), surplus.dtype), surplus[:-1]])
    return (BATCH + surplus - before).astype(jnp.int32)


def draw_positions(key, part):
    rows_drawn = jax.random.randint(jax.random.fold_in(key, 21), (SLOTS_ALL,), 0, TR)
    cols_drawn = jax.random.randint(jax.random.fold_in(key, 22), (SLOTS_ALL,), 0, OW - PS + 1)
    chosen = jax.random.randint(jax.random.fold_in(key, 23), (), 0, SLOTS_ALL)
    indices = jnp.arange(SLOTS_ALL)
    rows_drawn = jnp.where(indices == chosen, TR - 1, rows_drawn)
    cols_drawn = jnp.where(indices == chosen, OW - PS, cols_drawn)
    return jnp.stack([rows_drawn, cols_drawn], axis=1).astype(jnp.int32)


def block_scale(key, shape, shards, smallest, top_value):
    gain = 1.0
    for axis_at, blocks in shards:
        draws = jax.random.uniform(jax.random.fold_in(jax.random.fold_in(key, 6), axis_at), (blocks,), jnp.float32, smallest / len(shards), top_value / len(shards))
        gain = gain * jnp.repeat(jnp.exp(draws), shape[axis_at] // blocks).reshape((-1,) + (1,) * (len(shape) - 1 - axis_at))
    return gain


def scatter_about(rng, extent, scale, bound, shards=(), kind=jnp.bfloat16):
    entries = jax.random.normal(rng, extent, jnp.float32) * scale
    if len(shards) > 0:
        entries = block_scale(rng, extent, shards, -0.22, 0.18) * entries
    return jnp.clip(entries, min=-bound, max=bound).astype(kind)


def setup_inputs(seed: int = 0, part: int = 0) -> dict:
    streams_of = jax.random.split(jax.random.key(seed), 7)
    part_keys = jax.random.split(jax.random.fold_in(streams_of[6], part), 7)
    tile_object = scatter_about(part_keys[0], (NS, 2, OROWS, OW), 0.7, 6.0, ((2, 16),), jnp.float32)
    probe_wave = scatter_about(streams_of[1], (2, PS, PS), 0.7, 6.0, (), jnp.float32)
    propagator_phase = jnp.clip(jax.random.uniform(streams_of[2], (PS, PS), jnp.float32, -3.140625, 3.140625), -3.140625, 3.140625)
    diffraction = jnp.clip(2.0 * jax.random.uniform(part_keys[3], (SLOTS_ALL, PS, PS), jnp.float32) ** block_scale(part_keys[3], (SLOTS_ALL, PS, PS), ((0, 16),), -0.2, 0.2), 0.0, 2.0)
    positions = draw_positions(jax.random.fold_in(jax.random.fold_in(streams_of[6], part), 71), part)
    counts = draw_counts(jax.random.fold_in(jax.random.fold_in(streams_of[6], part), 71), part)
    return {"tile_object": tile_object, "probe_wave": probe_wave, "propagator_phase": propagator_phase, "diffraction": diffraction, "positions": positions, "counts": counts}


def exit_loss(patches, probe_wave, propagator_phase, pattern):
    wavefield = lax.complex(probe_wave[0], probe_wave[1])
    kernel = lax.complex(jnp.cos(propagator_phase), jnp.sin(propagator_phase))
    for layer_index in range(NS):
        wavefield = wavefield * lax.complex(patches[layer_index, 0], patches[layer_index, 1])
        if layer_index + 1 < NS:
            spectrum = jnp.fft.fft2(wavefield, norm='ortho')
            wavefield = jnp.fft.ifft2(kernel * spectrum, norm='ortho')
    farfield = jnp.fft.fft2(wavefield, norm='ortho')
    intensity = jnp.real(farfield) ** 2 + jnp.imag(farfield) ** 2
    return jnp.sum((intensity - pattern) ** 2)

def reference(tile_object, probe_wave, propagator_phase, diffraction, positions, counts):
    padded = jnp.concatenate([tile_object, tile_object[:, :, :PS]], axis=2)
    patch_gradient = jax.grad(exit_loss)
    anchor = jnp.zeros((), jnp.int32)

    def accumulate(summed, slot_number):
        holder = slot_number // SLOTS
        is_live = (slot_number % SLOTS < counts[holder]).astype(summed.dtype)
        row_start = (holder * TR + positions[slot_number, 0]).astype(jnp.int32)
        col_start = positions[slot_number, 1].astype(jnp.int32)
        corner = (anchor, anchor, row_start, col_start)
        patches = lax.dynamic_slice(padded, corner, (NS, 2, PS, PS))
        gradient = patch_gradient(patches, probe_wave, propagator_phase, diffraction[slot_number]) * is_live
        current = lax.dynamic_slice(summed, corner, (NS, 2, PS, PS))
        return (lax.dynamic_update_slice(summed, current + gradient, corner), None)
    summed, unused = lax.scan(accumulate, jnp.zeros_like(padded), jnp.arange(SLOTS_ALL, dtype=jnp.int32))
    top_rows = summed[:, :, :PS] + summed[:, :, OROWS:]
    return jnp.concatenate([top_rows, summed[:, :, PS:OROWS]], axis=2)
```

```python
import jax
import jax.numpy as jnp
import numpy as np
from jax import lax
from jax.experimental import pallas as pl
from jax.experimental.pallas import tpu as pltpu
from jax.sharding import PartitionSpec as P

PS = 128
NS = 4
BF = jnp.bfloat16
F32 = jnp.float32
VMEM = pl.BlockSpec(memory_space=pltpu.VMEM)
SMEM = pl.BlockSpec(memory_space=pltpu.SMEM)


def shifted(x, axis, by):
    peers = lax.axis_size(axis)
    return lax.ppermute(x, axis, [(i, (i + by) % peers) for i in range(peers)])


def dft_parts():
    k = np.arange(PS)
    ang = (np.outer(k, k) % PS) * (2.0 * np.pi / PS)
    c = np.cos(ang) / np.sqrt(PS)
    s = -np.sin(ang) / np.sqrt(PS)
    forward = np.block([[c, s], [-s, c]]).astype(np.float32)
    inverse = np.block([[c, -s], [s, c]]).astype(np.float32)
    parts = []
    for m in (forward, inverse):
        hi = m.astype(BF)
        lo = (m - hi.astype(np.float32)).astype(BF)
        parts += [hi, lo]
    return np.stack(parts)


def crop_kernel(pos, left_ref, right_ref, out_ref):
    s = pos[pl.program_id(0), 1] % PS
    lane = lax.broadcasted_iota(jnp.int32, (PS, PS), 1)
    for a in range(NS):
        for b in range(2):
            picked = jnp.where(lane >= s, left_ref[a, b], right_ref[a, b])
            out_ref[0, a, b] = pltpu.roll(picked, (PS - s) % PS, 1)


def crop(tile, positions):
    slots = positions.shape[0]
    last = tile.shape[3] // PS - 1
    block = (NS, 2, PS, PS)
    return pl.pallas_call(
        crop_kernel,
        grid_spec=pltpu.PrefetchScalarGridSpec(
            num_scalar_prefetch=1,
            grid=(slots,),
            in_specs=[
                pl.BlockSpec(block, lambda j, pos: (0, 0, 0, pos[j, 1] // PS)),
                pl.BlockSpec(block, lambda j, pos: (0, 0, 0, jnp.minimum(pos[j, 1] // PS + 1, last))),
            ],
            out_specs=pl.BlockSpec((1,) + block, lambda j, pos: (j, 0, 0, 0, 0)),
        ),
        out_shape=jax.ShapeDtypeStruct((slots,) + block, F32),
        cost_estimate=pl.CostEstimate(flops=10**6, bytes_accessed=6 * 10**6, transcendentals=0),
    )(positions, tile, tile)


def split(x):
    hi = x.astype(BF)
    return hi, (x - hi.astype(F32)).astype(BF)


def dot(a, b):
    return jnp.dot(a, b, preferred_element_type=F32)


def stack_rows(re, im):
    return jnp.concatenate([re, im], axis=0)


def to_rows(z):
    return jnp.concatenate(
        [
            jnp.concatenate([z[:PS, :PS], z[PS:, :PS]], axis=1),
            jnp.concatenate([z[:PS, PS:], z[PS:, PS:]], axis=1),
        ],
        axis=0,
    )


def grad_kernel(pos, counts, own_ref, low_ref, probe_ref, kre_ref, kim_ref, diff_ref, tab_ref, up_ref, down_ref, t_ref, w_ref):
    pairs = range(own_ref.shape[0] // 2)
    row = lax.broadcasted_iota(jnp.int32, (PS, PS), 0)

    def left(xs, inv):
        hi, lo = tab_ref[2 - 2 * inv], tab_ref[3 - 2 * inv]
        parts = [split(x) for x in xs]
        return [dot(hi, h) + dot(hi, l) + dot(lo, h) for h, l in parts]

    def right(xs, inv):
        hi, lo = tab_ref[2 * inv], tab_ref[2 * inv + 1]
        parts = [split(x) for x in xs]
        return [dot(h, hi) + dot(l, hi) + dot(h, lo) for h, l in parts]

    def forward(xs):
        return right([to_rows(x) for x in left(xs, 0)], 0)

    def backward(xs):
        return left([to_rows(x) for x in right(xs, 1)], 1)

    for p in pairs:
        for half in range(2):
            j = 2 * p + half
            p0 = pos[j, 0]
            for a in range(NS):
                for b in range(2):
                    picked = jnp.where(row >= p0, own_ref[j, a, b], low_ref[j, a, b])
                    t_ref[a, p, b, :, half * PS : (half + 1) * PS] = pltpu.roll(picked, (PS - p0) % PS, 0)
        for b in range(2):
            w_ref[0, p, b] = jnp.concatenate([probe_ref[b]] * 2, axis=1)

    def kernel_product(z, sign):
        kre = jnp.concatenate([kre_ref[...]] * 2, axis=0)
        kim = jnp.concatenate([kim_ref[...]] * 2, axis=0) * sign
        re, im = z[:, :PS], z[:, PS:]
        return jnp.concatenate([re * kre - im * kim, re * kim + im * kre], axis=1)

    def through(s):
        xs = []
        for p in pairs:
            wre, wim, tre, tim = w_ref[s, p, 0], w_ref[s, p, 1], t_ref[s, p, 0], t_ref[s, p, 1]
            xs.append(stack_rows(wre * tre - wim * tim, wre * tim + wim * tre))
        return xs

    def advance(s, carry):
        zs = [kernel_product(z, 1.0) for z in forward(through(s))]
        for p, x in zip(pairs, backward(zs)):
            w_ref[s + 1, p, 0] = x[:PS]
            w_ref[s + 1, p, 1] = x[PS:]
        return carry

    lax.fori_loop(0, NS - 1, advance, 0)

    gs = []
    for p, z in zip(pairs, forward(through(NS - 1))):
        halves = []
        for half in range(2):
            j = 2 * p + half
            live = jnp.where(j < counts[0], 4.0, 0.0).astype(F32)
            re, im = z[half * PS : (half + 1) * PS, :PS], z[half * PS : (half + 1) * PS, PS:]
            f = (re * re + im * im - diff_ref[j]) * live
            halves.append(jnp.concatenate([re * f, im * f], axis=1))
        gs.append(jnp.concatenate(halves, axis=0))
    gs = backward(gs)

    def deposit(s, gs):
        for p in pairs:
            gre, gim = gs[p][:PS], gs[p][PS:]
            wre, wim = w_ref[s, p, 0], w_ref[s, p, 1]
            for b, val in enumerate((wre * gre + wim * gim, wre * gim - wim * gre)):
                for half in range(2):
                    j = 2 * p + half
                    p0 = pos[j, 0]
                    v = pltpu.roll(val[:, half * PS : (half + 1) * PS], p0, 0)
                    up_ref[j, s, b] = jnp.where(row >= p0, v, 0.0)
                    down_ref[j, s, b] = jnp.where(row >= p0, 0.0, v)

    def retreat(i, gs):
        s = NS - 1 - i
        deposit(s, gs)
        xs = []
        for p in pairs:
            gre, gim = gs[p][:PS], gs[p][PS:]
            tre, tim = t_ref[s, p, 0], t_ref[s, p, 1]
            xs.append(stack_rows(gre * tre + gim * tim, gim * tre - gre * tim))
        return tuple(backward([kernel_product(z, -1.0) for z in forward(xs)]))

    gs = lax.fori_loop(0, NS - 1, retreat, tuple(gs))
    deposit(0, gs)


def gradients(own, low, probe, kre, kim, diff, positions, counts):
    slots = own.shape[0]
    out = jax.ShapeDtypeStruct(own.shape, F32)
    tables = jnp.asarray(dft_parts())
    return pl.pallas_call(
        grad_kernel,
        out_shape=(out, out),
        in_specs=[SMEM, SMEM] + [VMEM] * 7,
        out_specs=(VMEM, VMEM),
        scratch_shapes=[pltpu.VMEM((NS, slots // 2, 2, PS, 2 * PS), F32)] * 2,
        compiler_params=pltpu.CompilerParams(vmem_limit_bytes=48 << 20),
        cost_estimate=pl.CostEstimate(flops=6 * 10**9, bytes_accessed=9 * 10**6, transcendentals=0),
    )(positions, counts, own, low, probe, kre, kim, diff, tables)


def place_kernel(pos, before, up_ref, down_ref, out_ref, acc_ref):
    block = pl.program_id(0)
    lane = lax.broadcasted_iota(jnp.int32, (PS, PS), 1)
    acc_ref[...] = jnp.zeros_like(acc_ref)
    for source, where in ((up_ref, pos), (down_ref, before)):
        for j in range(up_ref.shape[0]):
            k, s = where[j, 1] // PS, where[j, 1] % PS
            ours = jnp.where(k == block, 1, 0)
            bound = jnp.where(ours == 1, s, 0)
            top = jnp.where(ours == 1, PS, s)

            @pl.when((k == block) | (k + 1 == block))
            def _():
                keep = (lane >= bound) & (lane < top)
                for a in range(NS):
                    for b in range(2):
                        acc_ref[a, b] += jnp.where(keep, pltpu.roll(source[j, a, b], s, 1), 0.0)

    out_ref[...] = acc_ref[...]


def place(up, down, positions, before, width):
    block = (NS, 2, PS, PS)
    return pl.pallas_call(
        place_kernel,
        grid_spec=pltpu.PrefetchScalarGridSpec(
            num_scalar_prefetch=2,
            grid=(width // PS,),
            in_specs=[VMEM, VMEM],
            out_specs=pl.BlockSpec(block, lambda b, *_: (0, 0, 0, b)),
            scratch_shapes=[pltpu.VMEM(block, F32)],
        ),
        out_shape=jax.ShapeDtypeStruct((NS, 2, PS, width), F32),
        compiler_params=pltpu.CompilerParams(vmem_limit_bytes=32 << 20),
        cost_estimate=pl.CostEstimate(flops=10**6, bytes_accessed=7 * 10**6, transcendentals=0),
    )(positions, before, up, down)


def per_device(tile_object, probe_wave, propagator_phase, diffraction, positions, counts):
    before = shifted(positions, "ty", 1)
    low = shifted(crop(tile_object, before), "ty", -1)
    own = crop(tile_object, positions)
    kre, kim = jnp.cos(propagator_phase), jnp.sin(propagator_phase)
    up, down = gradients(own, low, probe_wave, kre, kim, diffraction, positions, counts)
    return place(up, shifted(down, "ty", 1), positions, before, tile_object.shape[3])


def solution(mesh):
    in_specs = (
        P(None, None, ("grp", "ty"), None),
        P(),
        P(),
        P(("grp", "ty"), None, None),
        P(("grp", "ty"), None),
        P(("grp", "ty")),
    )
    out_specs = P(None, None, ("grp", "ty"), None)
    return jax.shard_map(
        per_device, mesh=mesh, in_specs=in_specs, out_specs=out_specs, check_vma=False
    )
```

```python
import jax
import jax.numpy as jnp
import numpy as np
from jax import lax
from jax.experimental import pallas as pl
from jax.experimental.pallas import tpu as pltpu
from jax.sharding import PartitionSpec as P

PS = 128
NS = 4
BF = jnp.bfloat16
F32 = jnp.float32
VMEM = pl.BlockSpec(memory_space=pltpu.VMEM)
SMEM = pl.BlockSpec(memory_space=pltpu.SMEM)


def shifted(x, axis, by):
    peers = lax.axis_size(axis)
    return lax.ppermute(x, axis, [(i, (i + by) % peers) for i in range(peers)])


def dft_parts():
    k = np.arange(PS)
    ang = (np.outer(k, k) % PS) * (2.0 * np.pi / PS)
    c = np.cos(ang) / np.sqrt(PS)
    s = -np.sin(ang) / np.sqrt(PS)
    forward = np.block([[c, s], [-s, c]]).astype(np.float32)
    inverse = np.block([[c, -s], [s, c]]).astype(np.float32)
    parts = []
    for m in (forward, inverse):
        hi = m.astype(BF)
        lo = (m - hi.astype(np.float32)).astype(BF)
        parts += [hi, lo]
    return np.stack(parts)


def crop_kernel(pos, left_ref, right_ref, out_ref):
    s = pos[pl.program_id(0), 1] % PS
    lane = lax.broadcasted_iota(jnp.int32, (PS, PS), 1)
    for a in range(NS):
        for b in range(2):
            picked = jnp.where(lane >= s, left_ref[a, b], right_ref[a, b])
            out_ref[0, a, b] = pltpu.roll(picked, (PS - s) % PS, 1)


def crop(tile, positions):
    slots = positions.shape[0]
    last = tile.shape[3] // PS - 1
    block = (NS, 2, PS, PS)
    return pl.pallas_call(
        crop_kernel,
        grid_spec=pltpu.PrefetchScalarGridSpec(
            num_scalar_prefetch=1,
            grid=(slots,),
            in_specs=[
                pl.BlockSpec(block, lambda j, pos: (0, 0, 0, pos[j, 1] // PS)),
                pl.BlockSpec(block, lambda j, pos: (0, 0, 0, jnp.minimum(pos[j, 1] // PS + 1, last))),
            ],
            out_specs=pl.BlockSpec((1,) + block, lambda j, pos: (j, 0, 0, 0, 0)),
        ),
        out_shape=jax.ShapeDtypeStruct((slots,) + block, F32),
        cost_estimate=pl.CostEstimate(flops=10**3, bytes_accessed=10**4, transcendentals=0),
    )(positions, tile, tile)


def split(x):
    hi = x.astype(BF)
    return hi, (x - hi.astype(F32)).astype(BF)


def dot(a, b):
    return jnp.dot(a, b, preferred_element_type=F32)


def stack_rows(re, im):
    return jnp.concatenate([re, im], axis=0)


def to_rows(z):
    return jnp.concatenate(
        [
            jnp.concatenate([z[:PS, :PS], z[PS:, :PS]], axis=1),
            jnp.concatenate([z[:PS, PS:], z[PS:, PS:]], axis=1),
        ],
        axis=0,
    )


def grad_kernel(pos, counts, own_ref, low_ref, probe_ref, kre_ref, kim_ref, diff_ref, tab_ref, up_ref, down_ref, t_ref, w_ref):
    pairs = range(own_ref.shape[0] // 2)
    row = lax.broadcasted_iota(jnp.int32, (PS, PS), 0)

    def left(xs, inv):
        hi, lo = tab_ref[2 - 2 * inv], tab_ref[3 - 2 * inv]
        parts = [split(x) for x in xs]
        return [dot(hi, h) + dot(hi, l) + dot(lo, h) for h, l in parts]

    def right(xs, inv):
        hi, lo = tab_ref[2 * inv], tab_ref[2 * inv + 1]
        parts = [split(x) for x in xs]
        return [dot(h, hi) + dot(l, hi) + dot(h, lo) for h, l in parts]

    def forward(xs):
        return right([to_rows(x) for x in left(xs, 0)], 0)

    def backward(xs):
        return left([to_rows(x) for x in right(xs, 1)], 1)

    for p in pairs:
        for half in range(2):
            j = 2 * p + half
            p0 = pos[j, 0]
            for a in range(NS):
                for b in range(2):
                    picked = jnp.where(row >= p0, own_ref[j, a, b], low_ref[j, a, b])
                    t_ref[a, p, b, :, half * PS : (half + 1) * PS] = pltpu.roll(picked, (PS - p0) % PS, 0)
        for b in range(2):
            w_ref[0, p, b] = jnp.concatenate([probe_ref[b]] * 2, axis=1)

    def kernel_product(z, sign):
        kre = jnp.concatenate([kre_ref[...]] * 2, axis=0)
        kim = jnp.concatenate([kim_ref[...]] * 2, axis=0) * sign
        re, im = z[:, :PS], z[:, PS:]
        return jnp.concatenate([re * kre - im * kim, re * kim + im * kre], axis=1)

    def through(s):
        xs = []
        for p in pairs:
            wre, wim, tre, tim = w_ref[s, p, 0], w_ref[s, p, 1], t_ref[s, p, 0], t_ref[s, p, 1]
            xs.append(stack_rows(wre * tre - wim * tim, wre * tim + wim * tre))
        return xs

    def advance(s, carry):
        zs = [kernel_product(z, 1.0) for z in forward(through(s))]
        for p, x in zip(pairs, backward(zs)):
            w_ref[s + 1, p, 0] = x[:PS]
            w_ref[s + 1, p, 1] = x[PS:]
        return carry

    lax.fori_loop(0, NS - 1, advance, 0)

    gs = []
    for p, z in zip(pairs, forward(through(NS - 1))):
        halves = []
        for half in range(2):
            j = 2 * p + half
            live = jnp.where(j < counts[0], 4.0, 0.0).astype(F32)
            re, im = z[half * PS : (half + 1) * PS, :PS], z[half * PS : (half + 1) * PS, PS:]
            f = (re * re + im * im - diff_ref[j]) * live
            halves.append(jnp.concatenate([re * f, im * f], axis=1))
        gs.append(jnp.concatenate(halves, axis=0))
    gs = backward(gs)

    def deposit(s, gs):
        for p in pairs:
            gre, gim = gs[p][:PS], gs[p][PS:]
            wre, wim = w_ref[s, p, 0], w_ref[s, p, 1]
            for b, val in enumerate((wre * gre + wim * gim, wre * gim - wim * gre)):
                for half in range(2):
                    j = 2 * p + half
                    p0 = pos[j, 0]
                    v = pltpu.roll(val[:, half * PS : (half + 1) * PS], p0, 0)
                    up_ref[j, s, b] = jnp.where(row >= p0, v, 0.0)
                    down_ref[j, s, b] = jnp.where(row >= p0, 0.0, v)

    def retreat(i, gs):
        s = NS - 1 - i
        deposit(s, gs)
        xs = []
        for p in pairs:
            gre, gim = gs[p][:PS], gs[p][PS:]
            tre, tim = t_ref[s, p, 0], t_ref[s, p, 1]
            xs.append(stack_rows(gre * tre + gim * tim, gim * tre - gre * tim))
        return tuple(backward([kernel_product(z, -1.0) for z in forward(xs)]))

    gs = lax.fori_loop(0, NS - 1, retreat, tuple(gs))
    deposit(0, gs)


def gradients(own, low, probe, kre, kim, diff, positions, counts):
    slots = own.shape[0]
    out = jax.ShapeDtypeStruct(own.shape, F32)
    tables = jnp.asarray(dft_parts())
    return pl.pallas_call(
        grad_kernel,
        out_shape=(out, out),
        in_specs=[SMEM, SMEM] + [VMEM] * 7,
        out_specs=(VMEM, VMEM),
        scratch_shapes=[pltpu.VMEM((NS, slots // 2, 2, PS, 2 * PS), F32)] * 2,
        compiler_params=pltpu.CompilerParams(vmem_limit_bytes=48 << 20),
        cost_estimate=pl.CostEstimate(flops=3 * 10**9, bytes_accessed=5 * 10**6, transcendentals=0),
    )(positions, counts, own, low, probe, kre, kim, diff, tables)


def place_kernel(where, *refs):
    *sources, out_ref, acc_ref = refs
    block = pl.program_id(0)
    lane = lax.broadcasted_iota(jnp.int32, (PS, PS), 1)
    if len(sources[0].shape) == 4:
        acc_ref[...] = sources.pop(0)[...]
    else:
        acc_ref[...] = jnp.zeros_like(acc_ref)
    row = 0
    for source in sources:
        for j in range(source.shape[0]):
            k, s = where[row, 1] // PS, where[row, 1] % PS
            row += 1
            bound = jnp.where(k == block, s, 0)
            top = jnp.where(k == block, PS, s)

            @pl.when((k == block) | (k + 1 == block))
            def _():
                keep = (lane >= bound) & (lane < top)
                for a in range(NS):
                    for b in range(2):
                        acc_ref[a, b] += jnp.where(keep, pltpu.roll(source[j, a, b], s, 1), 0.0)

    out_ref[...] = acc_ref[...]


def place(base, sources, where, width):
    block = (NS, 2, PS, PS)
    spec = pl.BlockSpec(block, lambda b, *_: (0, 0, 0, b))
    bases = [] if base is None else [base]
    return pl.pallas_call(
        place_kernel,
        grid_spec=pltpu.PrefetchScalarGridSpec(
            num_scalar_prefetch=1,
            grid=(width // PS,),
            in_specs=[spec] * len(bases) + [VMEM] * len(sources),
            out_specs=spec,
            scratch_shapes=[pltpu.VMEM(block, F32)],
        ),
        out_shape=jax.ShapeDtypeStruct((NS, 2, PS, width), F32),
        compiler_params=pltpu.CompilerParams(vmem_limit_bytes=32 << 20),
        cost_estimate=pl.CostEstimate(flops=10**6, bytes_accessed=7 * 10**6, transcendentals=0),
    )(where, *bases, *sources)


def per_device(tile_object, probe_wave, propagator_phase, diffraction, positions, counts):
    width = tile_object.shape[3]
    slots = positions.shape[0]
    before = shifted(positions, "ty", 1)
    first, rest = slice(0, slots // 2), slice(slots // 2, slots)
    low_a = shifted(crop(tile_object, before[first]), "ty", -1)
    own_a, own_b = crop(tile_object, positions[first]), crop(tile_object, positions[rest])
    where_b, own_a, own_b = lax.optimization_barrier((before[rest], own_a, own_b))
    rest_low, _ = lax.optimization_barrier((crop(tile_object, where_b), low_a))
    low_b = shifted(rest_low, "ty", -1)
    kre, kim = jnp.cos(propagator_phase), jnp.sin(propagator_phase)

    def pair(own, low, part, live):
        return gradients(own, low, probe_wave, kre, kim, diffraction[part], positions[part], live)

    up_a, down_a = pair(own_a, low_a, first, counts)
    down_a = shifted(down_a, "ty", 1)
    up_b, down_b = pair(own_b, low_b, rest, counts - slots // 2)
    down_b = shifted(down_b, "ty", 1)
    base = place(None, [up_a, up_b, down_a], jnp.concatenate([positions, before[first]], axis=0), width)
    return place(base, [down_b], before[rest], width)


def solution(mesh):
    in_specs = (
        P(None, None, ("grp", "ty"), None),
        P(),
        P(),
        P(("grp", "ty"), None, None),
        P(("grp", "ty"), None),
        P(("grp", "ty")),
    )
    out_specs = P(None, None, ("grp", "ty"), None)
    return jax.shard_map(
        per_device, mesh=mesh, in_specs=in_specs, out_specs=out_specs, check_vma=False
    )
```

```python
import jax
import jax.numpy as jnp
import numpy as np
from jax import lax
from jax.experimental import pallas as pl
from jax.experimental.pallas import tpu as pltpu
from jax.sharding import PartitionSpec as P

PS = 128
NS = 4
BF = jnp.bfloat16
F32 = jnp.float32
VMEM = pl.BlockSpec(memory_space=pltpu.VMEM)
SMEM = pl.BlockSpec(memory_space=pltpu.SMEM)


def shifted(x, axis, by):
    peers = lax.axis_size(axis)
    return lax.ppermute(x, axis, [(i, (i + by) % peers) for i in range(peers)])


def dft_parts():
    k = np.arange(PS)
    ang = (np.outer(k, k) % PS) * (2.0 * np.pi / PS)
    c = np.cos(ang) / np.sqrt(PS)
    s = -np.sin(ang) / np.sqrt(PS)
    forward = np.block([[c, s], [-s, c]]).astype(np.float32)
    inverse = np.block([[c, -s], [s, c]]).astype(np.float32)
    parts = []
    for m in (forward, inverse):
        hi = m.astype(BF)
        lo = (m - hi.astype(np.float32)).astype(BF)
        parts += [hi, lo]
    return np.stack(parts)


def crop_kernel(where, tile_ref, out_ref):
    last = tile_ref.shape[3] // PS - 1
    lane = lax.broadcasted_iota(jnp.int32, (PS, PS), 1)
    for j in range(out_ref.shape[0]):
        k, s = where[j, 1] // PS, where[j, 1] % PS
        here = pl.ds(pl.multiple_of(k * PS, PS), PS)
        after = pl.ds(pl.multiple_of(jnp.minimum(k + 1, last) * PS, PS), PS)
        for a in range(NS):
            for b in range(2):
                picked = jnp.where(lane >= s, tile_ref[a, b, :, here], tile_ref[a, b, :, after])
                out_ref[j, a, b] = pltpu.roll(picked, (PS - s) % PS, 1)


def crop(tile, where):
    return pl.pallas_call(
        crop_kernel,
        in_specs=[SMEM, VMEM],
        out_specs=VMEM,
        out_shape=jax.ShapeDtypeStruct((where.shape[0], NS, 2, PS, PS), F32),
        compiler_params=pltpu.CompilerParams(vmem_limit_bytes=8 << 20),
        cost_estimate=pl.CostEstimate(flops=10**3, bytes_accessed=10**4, transcendentals=0),
    )(where, tile)


def split(x):
    hi = x.astype(BF)
    return hi, (x - hi.astype(F32)).astype(BF)


def dot(a, b):
    return jnp.dot(a, b, preferred_element_type=F32)


def grad_kernel(pos, counts, own_ref, low_ref, probe_ref, kre_ref, kim_ref, diff_ref, tab_ref, up_ref, down_ref, t_ref, w_ref):
    slots = range(own_ref.shape[0])
    row = lax.broadcasted_iota(jnp.int32, (PS, PS), 0)

    def left(zs, inv):
        hi, lo = tab_ref[2 - 2 * inv], tab_ref[3 - 2 * inv]
        parts = [split(jnp.concatenate(z, axis=0)) for z in zs]
        ys = [dot(hi, h) + dot(hi, l) + dot(lo, h) for h, l in parts]
        return [(y[:PS], y[PS:]) for y in ys]

    def right(zs, inv):
        hi, lo = tab_ref[2 * inv], tab_ref[2 * inv + 1]
        parts = [split(jnp.concatenate(z, axis=1)) for z in zs]
        ys = [dot(h, hi) + dot(l, hi) + dot(h, lo) for h, l in parts]
        return [(y[:, :PS], y[:, PS:]) for y in ys]

    def forward(zs):
        return right(left(zs, 0), 0)

    def backward(zs):
        return left(right(zs, 1), 1)

    for j in slots:
        p0 = pos[j, 0]
        for a in range(NS):
            for b in range(2):
                picked = jnp.where(row >= p0, own_ref[j, a, b], low_ref[j, a, b])
                t_ref[a, j, b] = pltpu.roll(picked, (PS - p0) % PS, 0)
        for b in range(2):
            w_ref[0, j, b] = probe_ref[b]

    def kernel_product(z, sign):
        re, im = z
        kre, kim = kre_ref[...], kim_ref[...] * sign
        return re * kre - im * kim, re * kim + im * kre

    def through(s):
        zs = []
        for j in slots:
            wre, wim, tre, tim = w_ref[s, j, 0], w_ref[s, j, 1], t_ref[s, j, 0], t_ref[s, j, 1]
            zs.append((wre * tre - wim * tim, wre * tim + wim * tre))
        return zs

    def advance(s, carry):
        zs = [kernel_product(z, 1.0) for z in forward(through(s))]
        for j, z in zip(slots, backward(zs)):
            w_ref[s + 1, j, 0], w_ref[s + 1, j, 1] = z
        return carry

    lax.fori_loop(0, NS - 1, advance, 0)

    gs = []
    for j, (re, im) in zip(slots, forward(through(NS - 1))):
        live = jnp.where(j < counts[0], 4.0, 0.0).astype(F32)
        f = (re * re + im * im - diff_ref[j]) * live
        gs.append((re * f, im * f))
    gs = backward(gs)

    def deposit(s, gs):
        for j, (gre, gim) in zip(slots, gs):
            p0 = pos[j, 0]
            wre, wim = w_ref[s, j, 0], w_ref[s, j, 1]
            for b, val in enumerate((wre * gre + wim * gim, wre * gim - wim * gre)):
                v = pltpu.roll(val, p0, 0)
                up_ref[j, s, b] = jnp.where(row >= p0, v, 0.0)
                down_ref[j, s, b] = jnp.where(row >= p0, 0.0, v)

    def retreat(i, gs):
        s = NS - 1 - i
        deposit(s, gs)
        zs = []
        for j, (gre, gim) in zip(slots, gs):
            tre, tim = t_ref[s, j, 0], t_ref[s, j, 1]
            zs.append((gre * tre + gim * tim, gim * tre - gre * tim))
        return tuple(backward([kernel_product(z, -1.0) for z in forward(zs)]))

    gs = lax.fori_loop(0, NS - 1, retreat, tuple(gs))
    deposit(0, gs)


def gradients(own, low, probe, kre, kim, diff, positions, counts):
    slots = own.shape[0]
    out = jax.ShapeDtypeStruct(own.shape, F32)
    tables = jnp.asarray(dft_parts())
    return pl.pallas_call(
        grad_kernel,
        out_shape=(out, out),
        in_specs=[SMEM, SMEM] + [VMEM] * 7,
        out_specs=(VMEM, VMEM),
        scratch_shapes=[pltpu.VMEM((NS, slots, 2, PS, PS), F32)] * 2,
        compiler_params=pltpu.CompilerParams(vmem_limit_bytes=12 << 20),
        cost_estimate=pl.CostEstimate(flops=3 * 10**9, bytes_accessed=5 * 10**6, transcendentals=0),
    )(positions, counts, own, low, probe, kre, kim, diff, tables)


def place_kernel(where, *refs):
    *sources, out_ref = refs
    last = out_ref.shape[3] // PS - 1
    lane = lax.broadcasted_iota(jnp.int32, (PS, PS), 1)
    if len(sources[0].shape) == 4:
        out_ref[...] = sources.pop(0)[...]
    else:
        out_ref[...] = jnp.zeros_like(out_ref)
    row = 0
    for source in sources:
        for j in range(source.shape[0]):
            k, s = where[row, 1] // PS, where[row, 1] % PS
            row += 1
            here = pl.ds(pl.multiple_of(k * PS, PS), PS)
            after = pl.ds(pl.multiple_of(jnp.minimum(k + 1, last) * PS, PS), PS)
            for a in range(NS):
                for b in range(2):
                    moved = pltpu.roll(source[j, a, b], s, 1)
                    out_ref[a, b, :, here] += jnp.where(lane >= s, moved, 0.0)
                    out_ref[a, b, :, after] += jnp.where(lane >= s, 0.0, moved)


def place(base, sources, where, width):
    bases = [] if base is None else [base]
    return pl.pallas_call(
        place_kernel,
        in_specs=[SMEM] + [VMEM] * (len(bases) + len(sources)),
        out_specs=VMEM,
        out_shape=jax.ShapeDtypeStruct((NS, 2, PS, width), F32),
        compiler_params=pltpu.CompilerParams(vmem_limit_bytes=12 << 20),
        cost_estimate=pl.CostEstimate(flops=10**6, bytes_accessed=7 * 10**6, transcendentals=0),
    )(where, *bases, *sources)


def per_device(tile_object, probe_wave, propagator_phase, diffraction, positions, counts):
    width = tile_object.shape[3]
    slots = positions.shape[0]
    before = shifted(positions, "ty", 1)
    first, rest = slice(0, slots // 2), slice(slots // 2, slots)
    low_a = shifted(crop(tile_object, before[first]), "ty", -1)
    own_a, own_b = crop(tile_object, positions[first]), crop(tile_object, positions[rest])
    where_b, own_a, own_b = lax.optimization_barrier((before[rest], own_a, own_b))
    rest_low, _ = lax.optimization_barrier((crop(tile_object, where_b), low_a))
    low_b = shifted(rest_low, "ty", -1)
    kre, kim = jnp.cos(propagator_phase), jnp.sin(propagator_phase)

    def pair(own, low, part, live):
        return gradients(own, low, probe_wave, kre, kim, diffraction[part], positions[part], live)

    up_a, down_a = pair(own_a, low_a, first, counts)
    down_a = shifted(down_a, "ty", 1)
    up_b, down_b = pair(own_b, low_b, rest, counts - slots // 2)
    down_b = shifted(down_b, "ty", 1)
    base = place(None, [up_a, up_b, down_a], jnp.concatenate([positions, before[first]], axis=0), width)
    return place(base, [down_b], before[rest], width)


def solution(mesh):
    in_specs = (
        P(None, None, ("grp", "ty"), None),
        P(),
        P(),
        P(("grp", "ty"), None, None),
        P(("grp", "ty"), None),
        P(("grp", "ty")),
    )
    out_specs = P(None, None, ("grp", "ty"), None)
    return jax.shard_map(
        per_device, mesh=mesh, in_specs=in_specs, out_specs=out_specs, check_vma=False
    )
```

```python
import functools

import jax
import jax.numpy as jnp
import numpy as np
from jax import lax
from jax.experimental import pallas as pl
from jax.experimental.pallas import tpu as pltpu
from jax.sharding import PartitionSpec as P

PS = 128
NS = 4
BF = jnp.bfloat16
F32 = jnp.float32
VMEM = pl.BlockSpec(memory_space=pltpu.VMEM)
SMEM = pl.BlockSpec(memory_space=pltpu.SMEM)


def shifted(x, axis, by):
    peers = lax.axis_size(axis)
    return lax.ppermute(x, axis, [(i, (i + by) % peers) for i in range(peers)])


def dft_parts():
    k = np.arange(PS)
    ang = (np.outer(k, k) % PS) * (2.0 * np.pi / PS)
    c = np.cos(ang) / np.sqrt(PS)
    s = -np.sin(ang) / np.sqrt(PS)
    forward = np.block([[c, s], [-s, c]]).astype(np.float32)
    inverse = np.block([[c, -s], [s, c]]).astype(np.float32)
    parts = []
    for m in (forward, inverse):
        hi = m.astype(BF)
        lo = (m - hi.astype(np.float32)).astype(BF)
        parts += [hi, lo]
    return np.stack(parts)


def crop_kernel(start, where, tile_ref, out_ref):
    last = tile_ref.shape[3] // PS - 1
    lane = lax.broadcasted_iota(jnp.int32, (PS, PS), 1)
    for j in range(out_ref.shape[0]):
        k, s = where[start + j, 1] // PS, where[start + j, 1] % PS
        here = pl.ds(pl.multiple_of(k * PS, PS), PS)
        after = pl.ds(pl.multiple_of(jnp.minimum(k + 1, last) * PS, PS), PS)
        for a in range(NS):
            for b in range(2):
                picked = jnp.where(lane >= s, tile_ref[a, b, :, here], tile_ref[a, b, :, after])
                out_ref[j, a, b] = pltpu.roll(picked, (PS - s) % PS, 1)


def crop(tile, where, start, stop):
    return pl.pallas_call(
        functools.partial(crop_kernel, start),
        in_specs=[SMEM, VMEM],
        out_specs=VMEM,
        out_shape=jax.ShapeDtypeStruct((stop - start, NS, 2, PS, PS), F32),
        compiler_params=pltpu.CompilerParams(vmem_limit_bytes=8 << 20),
        cost_estimate=pl.CostEstimate(flops=10**3, bytes_accessed=10**4, transcendentals=0),
    )(where, tile)


def split(x):
    hi = x.astype(BF)
    return hi, (x - hi.astype(F32)).astype(BF)


def dot(a, b):
    return jnp.dot(a, b, preferred_element_type=F32)


def grad_kernel(start, pos, counts, own_ref, low_ref, probe_ref, kre_ref, kim_ref, diff_ref, tab_ref, up_ref, down_ref, t_ref, w_ref):
    slots = range(own_ref.shape[0])
    row = lax.broadcasted_iota(jnp.int32, (PS, PS), 0)

    def left(zs, inv):
        hi, lo = tab_ref[2 - 2 * inv], tab_ref[3 - 2 * inv]
        parts = [split(jnp.concatenate(z, axis=0)) for z in zs]
        ys = [dot(hi, h) + dot(hi, l) + dot(lo, h) for h, l in parts]
        return [(y[:PS], y[PS:]) for y in ys]

    def right(zs, inv):
        hi, lo = tab_ref[2 * inv], tab_ref[2 * inv + 1]
        parts = [split(jnp.concatenate(z, axis=1)) for z in zs]
        ys = [dot(h, hi) + dot(l, hi) + dot(h, lo) for h, l in parts]
        return [(y[:, :PS], y[:, PS:]) for y in ys]

    def forward(zs):
        return right(left(zs, 0), 0)

    def backward(zs):
        return left(right(zs, 1), 1)

    for j in slots:
        p0 = pos[start + j, 0]
        for a in range(NS):
            for b in range(2):
                picked = jnp.where(row >= p0, own_ref[j, a, b], low_ref[j, a, b])
                t_ref[a, j, b] = pltpu.roll(picked, (PS - p0) % PS, 0)
        for b in range(2):
            w_ref[0, j, b] = probe_ref[b]

    def kernel_product(z, sign):
        re, im = z
        kre, kim = kre_ref[...], kim_ref[...] * sign
        return re * kre - im * kim, re * kim + im * kre

    def through(s):
        zs = []
        for j in slots:
            wre, wim, tre, tim = w_ref[s, j, 0], w_ref[s, j, 1], t_ref[s, j, 0], t_ref[s, j, 1]
            zs.append((wre * tre - wim * tim, wre * tim + wim * tre))
        return zs

    def advance(s, carry):
        zs = [kernel_product(z, 1.0) for z in forward(through(s))]
        for j, z in zip(slots, backward(zs)):
            w_ref[s + 1, j, 0], w_ref[s + 1, j, 1] = z
        return carry

    lax.fori_loop(0, NS - 1, advance, 0)

    gs = []
    for j, (re, im) in zip(slots, forward(through(NS - 1))):
        live = jnp.where(start + j < counts[0], 4.0, 0.0).astype(F32)
        f = (re * re + im * im - diff_ref[start + j]) * live
        gs.append((re * f, im * f))
    gs = backward(gs)

    def deposit(s, gs):
        for j, (gre, gim) in zip(slots, gs):
            p0 = pos[start + j, 0]
            wre, wim = w_ref[s, j, 0], w_ref[s, j, 1]
            for b, val in enumerate((wre * gre + wim * gim, wre * gim - wim * gre)):
                v = pltpu.roll(val, p0, 0)
                up_ref[j, s, b] = jnp.where(row >= p0, v, 0.0)
                down_ref[j, s, b] = jnp.where(row >= p0, 0.0, v)

    def retreat(i, gs):
        s = NS - 1 - i
        deposit(s, gs)
        zs = []
        for j, (gre, gim) in zip(slots, gs):
            tre, tim = t_ref[s, j, 0], t_ref[s, j, 1]
            zs.append((gre * tre + gim * tim, gim * tre - gre * tim))
        return tuple(backward([kernel_product(z, -1.0) for z in forward(zs)]))

    gs = lax.fori_loop(0, NS - 1, retreat, tuple(gs))
    deposit(0, gs)


def gradients(own, low, probe, kre, kim, diff, positions, counts, start):
    slots = own.shape[0]
    out = jax.ShapeDtypeStruct(own.shape, F32)
    tables = jnp.asarray(dft_parts())
    return pl.pallas_call(
        functools.partial(grad_kernel, start),
        out_shape=(out, out),
        in_specs=[SMEM, SMEM] + [VMEM] * 7,
        out_specs=(VMEM, VMEM),
        scratch_shapes=[pltpu.VMEM((NS, slots, 2, PS, PS), F32)] * 2,
        compiler_params=pltpu.CompilerParams(vmem_limit_bytes=12 << 20),
        cost_estimate=pl.CostEstimate(flops=3 * 10**9, bytes_accessed=5 * 10**6, transcendentals=0),
    )(positions, counts, own, low, probe, kre, kim, diff, tables)


def put(out_ref, source, j, where):
    last = out_ref.shape[3] // PS - 1
    lane = lax.broadcasted_iota(jnp.int32, (PS, PS), 1)
    k, s = where[1] // PS, where[1] % PS
    here = pl.ds(pl.multiple_of(k * PS, PS), PS)
    after = pl.ds(pl.multiple_of(jnp.minimum(k + 1, last) * PS, PS), PS)
    for a in range(out_ref.shape[0]):
        for b in range(2):
            moved = pltpu.roll(source[j, a, b], s, 1)
            out_ref[a, b, :, here] += jnp.where(lane >= s, moved, 0.0)
            out_ref[a, b, :, after] += jnp.where(lane >= s, 0.0, moved)


def first_kernel(pos, before, up_a_ref, up_b_ref, down_ref, out_ref):
    out_ref[...] = jnp.zeros_like(out_ref)
    half = down_ref.shape[0]
    for j in range(half):
        put(out_ref, up_a_ref, j, (pos[j, 0], pos[j, 1]))
        put(out_ref, up_b_ref, j, (pos[half + j, 0], pos[half + j, 1]))
        put(out_ref, down_ref, j, (before[j, 0], before[j, 1]))


def place_first(sources, positions, before, width):
    return pl.pallas_call(
        first_kernel,
        in_specs=[SMEM] * 2 + [VMEM] * len(sources),
        out_specs=VMEM,
        out_shape=jax.ShapeDtypeStruct((NS, 2, PS, width), F32),
        compiler_params=pltpu.CompilerParams(vmem_limit_bytes=12 << 20),
        cost_estimate=pl.CostEstimate(flops=10**6, bytes_accessed=7 * 10**6, transcendentals=0),
    )(positions, before, *sources)


def last_kernel(start, before, base_ref, down_ref, out_ref):
    out_ref[...] = base_ref[...]
    for j in range(down_ref.shape[0]):
        put(out_ref, down_ref, j, (before[start + j, 0], before[start + j, 1]))


def place_last(base, down, before, start):
    width = base.shape[3]
    spec = pl.BlockSpec((1, 2, PS, width), lambda a, *_: (a, 0, 0, 0))
    return pl.pallas_call(
        functools.partial(last_kernel, start),
        grid_spec=pltpu.PrefetchScalarGridSpec(
            num_scalar_prefetch=1,
            grid=(NS,),
            in_specs=[spec, pl.BlockSpec((down.shape[0], 1, 2, PS, PS), lambda a, *_: (0, a, 0, 0, 0))],
            out_specs=spec,
        ),
        out_shape=jax.ShapeDtypeStruct(base.shape, F32),
        compiler_params=pltpu.CompilerParams(vmem_limit_bytes=12 << 20),
        cost_estimate=pl.CostEstimate(flops=10**6, bytes_accessed=7 * 10**6, transcendentals=0),
    )(before, base, down)


def per_device(tile_object, probe_wave, propagator_phase, diffraction, positions, counts):
    width = tile_object.shape[3]
    slots = positions.shape[0]
    half = slots // 2
    before = shifted(positions, "ty", 1)
    low_a = shifted(crop(tile_object, before, 0, half), "ty", -1)
    kre, kim = jnp.cos(propagator_phase), jnp.sin(propagator_phase)
    low_b = shifted(crop(tile_object, before, half, slots), "ty", -1)
    own_a, own_b = crop(tile_object, positions, 0, half), crop(tile_object, positions, half, slots)

    def pair(own, low, start):
        return gradients(own, low, probe_wave, kre, kim, diffraction, positions, counts, start)

    up_a, down_a = pair(own_a, low_a, 0)
    down_a = shifted(down_a, "ty", 1)
    up_b, down_b = pair(own_b, low_b, half)
    down_b = shifted(down_b, "ty", 1)
    base = place_first([up_a, up_b, down_a], positions, before, width)
    return place_last(base, down_b, before, half)


def solution(mesh):
    in_specs = (
        P(None, None, ("grp", "ty"), None),
        P(),
        P(),
        P(("grp", "ty"), None, None),
        P(("grp", "ty"), None),
        P(("grp", "ty")),
    )
    out_specs = P(None, None, ("grp", "ty"), None)
    return jax.shard_map(
        per_device, mesh=mesh, in_specs=in_specs, out_specs=out_specs, check_vma=False
    )
```

```python
import functools

import jax
import jax.numpy as jnp
import numpy as np
from jax import lax
from jax.experimental import pallas as pl
from jax.experimental.pallas import tpu as pltpu
from jax.sharding import PartitionSpec as P

PS = 128
NS = 4
BF = jnp.bfloat16
F32 = jnp.float32
VMEM = pl.BlockSpec(memory_space=pltpu.VMEM)
SMEM = pl.BlockSpec(memory_space=pltpu.SMEM)


def shifted(x, axis, by):
    peers = lax.axis_size(axis)
    return lax.ppermute(x, axis, [(i, (i + by) % peers) for i in range(peers)])


def dft_parts():
    k = np.arange(PS)
    ang = (np.outer(k, k) % PS) * (2.0 * np.pi / PS)
    c = np.cos(ang) / np.sqrt(PS)
    s = -np.sin(ang) / np.sqrt(PS)
    forward = np.block([[c, s], [-s, c]]).astype(np.float32)
    inverse = np.block([[c, -s], [s, c]]).astype(np.float32)
    parts = []
    for m in (forward, inverse):
        hi = m.astype(BF)
        lo = (m - hi.astype(np.float32)).astype(BF)
        parts += [hi, lo]
    return np.stack(parts)


def crop_kernel(start, where, tile_ref, out_ref):
    last = tile_ref.shape[3] // PS - 1
    lane = lax.broadcasted_iota(jnp.int32, (PS, PS), 1)
    for j in range(out_ref.shape[0]):
        k, s = where[start + j, 1] // PS, where[start + j, 1] % PS
        here = pl.ds(pl.multiple_of(k * PS, PS), PS)
        after = pl.ds(pl.multiple_of(jnp.minimum(k + 1, last) * PS, PS), PS)
        for a in range(NS):
            for b in range(2):
                picked = jnp.where(lane >= s, tile_ref[a, b, :, here], tile_ref[a, b, :, after])
                out_ref[j, a, b] = pltpu.roll(picked, (PS - s) % PS, 1)


def crop(tile, where, start, stop):
    return pl.pallas_call(
        functools.partial(crop_kernel, start),
        in_specs=[SMEM, VMEM],
        out_specs=VMEM,
        out_shape=jax.ShapeDtypeStruct((stop - start, NS, 2, PS, PS), F32),
        compiler_params=pltpu.CompilerParams(vmem_limit_bytes=8 << 20),
        cost_estimate=pl.CostEstimate(flops=10**3, bytes_accessed=10**4, transcendentals=0),
    )(where, tile)


def split(x):
    hi = x.astype(BF)
    return hi, (x - hi.astype(F32)).astype(BF)


def dot(a, b):
    return jnp.dot(a, b, preferred_element_type=F32)


def grad_kernel(start, pos, counts, own_ref, low_ref, probe_ref, kre_ref, kim_ref, diff_ref, tab_ref, up_ref, down_ref, t_ref, w_ref):
    slots = range(low_ref.shape[0])
    row = lax.broadcasted_iota(jnp.int32, (PS, PS), 0)

    def left(zs, inv):
        hi, lo = tab_ref[2 - 2 * inv], tab_ref[3 - 2 * inv]
        parts = [split(jnp.concatenate(z, axis=0)) for z in zs]
        ys = [dot(hi, h) + dot(hi, l) + dot(lo, h) for h, l in parts]
        return [(y[:PS], y[PS:]) for y in ys]

    def right(zs, inv):
        hi, lo = tab_ref[2 * inv], tab_ref[2 * inv + 1]
        parts = [split(jnp.concatenate(z, axis=1)) for z in zs]
        ys = [dot(h, hi) + dot(l, hi) + dot(h, lo) for h, l in parts]
        return [(y[:, :PS], y[:, PS:]) for y in ys]

    def forward(zs):
        return right(left(zs, 0), 0)

    def backward(zs):
        return left(right(zs, 1), 1)

    for j in slots:
        p0 = pos[start + j, 0]
        for a in range(NS):
            for b in range(2):
                picked = jnp.where(row >= p0, own_ref[start + j, a, b], low_ref[j, a, b])
                t_ref[a, j, b] = pltpu.roll(picked, (PS - p0) % PS, 0)
        for b in range(2):
            w_ref[0, j, b] = probe_ref[b]

    def kernel_product(z, sign):
        re, im = z
        kre, kim = kre_ref[...], kim_ref[...] * sign
        return re * kre - im * kim, re * kim + im * kre

    def through(s):
        zs = []
        for j in slots:
            wre, wim, tre, tim = w_ref[s, j, 0], w_ref[s, j, 1], t_ref[s, j, 0], t_ref[s, j, 1]
            zs.append((wre * tre - wim * tim, wre * tim + wim * tre))
        return zs

    def advance(s, carry):
        zs = [kernel_product(z, 1.0) for z in forward(through(s))]
        for j, z in zip(slots, backward(zs)):
            w_ref[s + 1, j, 0], w_ref[s + 1, j, 1] = z
        return carry

    lax.fori_loop(0, NS - 1, advance, 0)

    gs = []
    for j, (re, im) in zip(slots, forward(through(NS - 1))):
        live = jnp.where(start + j < counts[0], 4.0, 0.0).astype(F32)
        f = (re * re + im * im - diff_ref[start + j]) * live
        gs.append((re * f, im * f))
    gs = backward(gs)

    def deposit(s, gs):
        for j, (gre, gim) in zip(slots, gs):
            p0 = pos[start + j, 0]
            wre, wim = w_ref[s, j, 0], w_ref[s, j, 1]
            for b, val in enumerate((wre * gre + wim * gim, wre * gim - wim * gre)):
                v = pltpu.roll(val, p0, 0)
                up_ref[j, s, b] = jnp.where(row >= p0, v, 0.0)
                down_ref[j, s, b] = jnp.where(row >= p0, 0.0, v)

    def retreat(i, gs):
        s = NS - 1 - i
        deposit(s, gs)
        zs = []
        for j, (gre, gim) in zip(slots, gs):
            tre, tim = t_ref[s, j, 0], t_ref[s, j, 1]
            zs.append((gre * tre + gim * tim, gim * tre - gre * tim))
        return tuple(backward([kernel_product(z, -1.0) for z in forward(zs)]))

    gs = lax.fori_loop(0, NS - 1, retreat, tuple(gs))
    deposit(0, gs)


def gradients(own, low, probe, kre, kim, diff, positions, counts, start):
    slots = low.shape[0]
    out = jax.ShapeDtypeStruct(low.shape, F32)
    tables = jnp.asarray(dft_parts())
    return pl.pallas_call(
        functools.partial(grad_kernel, start),
        out_shape=(out, out),
        in_specs=[SMEM, SMEM] + [VMEM] * 7,
        out_specs=(VMEM, VMEM),
        scratch_shapes=[pltpu.VMEM((NS, slots, 2, PS, PS), F32)] * 2,
        compiler_params=pltpu.CompilerParams(vmem_limit_bytes=12 << 20),
        cost_estimate=pl.CostEstimate(flops=2 * 10**9, bytes_accessed=3 * 10**6, transcendentals=0),
    )(positions, counts, own, low, probe, kre, kim, diff, tables)


def put(out_ref, source, j, where):
    last = out_ref.shape[3] // PS - 1
    lane = lax.broadcasted_iota(jnp.int32, (PS, PS), 1)
    k, s = where[1] // PS, where[1] % PS
    here = pl.ds(pl.multiple_of(k * PS, PS), PS)
    after = pl.ds(pl.multiple_of(jnp.minimum(k + 1, last) * PS, PS), PS)
    for a in range(out_ref.shape[0]):
        for b in range(2):
            moved = pltpu.roll(source[j, a, b], s, 1)
            out_ref[a, b, :, here] += jnp.where(lane >= s, moved, 0.0)
            out_ref[a, b, :, after] += jnp.where(lane >= s, 0.0, moved)


def first_kernel(n_ups, pos, before, *refs):
    *sources, out_ref = refs
    out_ref[...] = jnp.zeros_like(out_ref)
    for parts, where in ((sources[:n_ups], pos), (sources[n_ups:], before)):
        row = 0
        for source in parts:
            for j in range(source.shape[0]):
                put(out_ref, source, j, (where[row, 0], where[row, 1]))
                row += 1


def place_first(ups, downs, positions, before, width):
    return pl.pallas_call(
        functools.partial(first_kernel, len(ups)),
        in_specs=[SMEM] * 2 + [VMEM] * len(ups + downs),
        out_specs=VMEM,
        out_shape=jax.ShapeDtypeStruct((NS, 2, PS, width), F32),
        compiler_params=pltpu.CompilerParams(vmem_limit_bytes=12 << 20),
        cost_estimate=pl.CostEstimate(flops=10**6, bytes_accessed=7 * 10**6, transcendentals=0),
    )(positions, before, *ups, *downs)


def last_kernel(start, before, base_ref, down_ref, out_ref):
    out_ref[...] = base_ref[...]
    for j in range(down_ref.shape[0]):
        put(out_ref, down_ref, j, (before[start + j, 0], before[start + j, 1]))


def place_last(base, down, before, start):
    width = base.shape[3]
    spec = pl.BlockSpec((1, 2, PS, width), lambda a, *_: (a, 0, 0, 0))
    return pl.pallas_call(
        functools.partial(last_kernel, start),
        grid_spec=pltpu.PrefetchScalarGridSpec(
            num_scalar_prefetch=1,
            grid=(NS,),
            in_specs=[spec, pl.BlockSpec((down.shape[0], 1, 2, PS, PS), lambda a, *_: (0, a, 0, 0, 0))],
            out_specs=spec,
        ),
        out_shape=jax.ShapeDtypeStruct(base.shape, F32),
        compiler_params=pltpu.CompilerParams(vmem_limit_bytes=12 << 20),
        cost_estimate=pl.CostEstimate(flops=10**6, bytes_accessed=7 * 10**6, transcendentals=0),
    )(before, base, down)


def per_device(tile_object, probe_wave, propagator_phase, diffraction, positions, counts):
    width = tile_object.shape[3]
    slots = positions.shape[0]
    groups = [(j, j + 1) for j in range(slots)]
    own = crop(tile_object, positions, 0, slots)
    before, own = lax.optimization_barrier((shifted(positions, "ty", 1), own))
    lows = [shifted(crop(tile_object, before, *group), "ty", -1) for group in groups]
    kre, kim = jnp.cos(propagator_phase), jnp.sin(propagator_phase)
    ups, downs = [], []
    for (start, stop), low in zip(groups, lows):
        up, down = gradients(own, low, probe_wave, kre, kim, diffraction, positions, counts, start)
        ups.append(up)
        downs.append(shifted(down, "ty", 1))
    base = place_first(ups, downs[:-1], positions, before, width)
    return place_last(base, downs[-1], before, groups[-1][0])


def solution(mesh):
    in_specs = (
        P(None, None, ("grp", "ty"), None),
        P(),
        P(),
        P(("grp", "ty"), None, None),
        P(("grp", "ty"), None),
        P(("grp", "ty")),
    )
    out_specs = P(None, None, ("grp", "ty"), None)
    return jax.shard_map(
        per_device, mesh=mesh, in_specs=in_specs, out_specs=out_specs, check_vma=False
    )
```
